32 devices in a mesh: seq: 8 (over z, y), head: 4 (over x, core).
Axes of the slice: x: 2, y: 2, z: 4, core: 2. Of those that a mesh axis runs over, the one named last changes fastest.
Arguments:
- queries: bfloat16 [2, 64, 64, 128], P(None, 'head'), may hold values from -9 to 9
- cache_keys: bfloat16 [2, 8, 8192, 128], P(None, 'head', 'seq'), may hold values from -10 to 10
- cache_values: bfloat16 [2, 8, 8192, 128], P(None, 'head', 'seq'), may hold values from -6 to 6
- new_keys: bfloat16 [2, 8, 64, 128], P(None, 'head'), may hold values from -20 to 20
- new_values: bfloat16 [2, 8, 64, 128], P(None, 'head'), may hold values from -6 to 6
- parents: int32 [2, 64], replicated, may hold values from 0 to 62, as said below
- path: int32 [2, 6], replicated, may hold values from 0 to 63, as said below
- lengths: int32 [2], replicated, may hold values from 2048 to 8192, as said below
- draft_tokens: int32 [2, 64], replicated, may hold values from 0 to 65535
- residual: bfloat16 [2, 64, 8192], P(None, None, 'seq'), may hold values from -8 to 8
- out_weight: bfloat16 [8192, 8192], P('head', 'seq'), may hold values from -0.0625 to 0.0625
- norm_gain: bfloat16 [8192], P('seq'), may hold values from 0.5 to 1.5
- vocab_weight: bfloat16 [8192, 65536], P(None, ('seq', 'head')), may hold values from -3 to 3
Outputs:
- path_logits: float32 [2, 6, 65536], P(None, None, ('seq', 'head'))
- draft_logprob: float32 [2, 64], replicated
The draws below stay inside these ranges and needn't reach their ends.
Inputs may be any that keep to these rules, and one draw needn't show every extreme that they name: parents[b, 0] is 0; for every other node n, parents[b, n] is a smaller node number. path[b] lists 6 different nodes: node 0 first, and each later entry is a child (by parents) of the entry before it. `lengths`: at least one sequence uses all 8192 cache positions.
All inputs are finite; a program needn't handle non-finite values.
Results may differ from the reference program's by a relative error of at most 0.006.
Values may be sent and summed in bfloat16 or wider, within the bound.
A program may use at most 128 MiB of HBM per device.

```python
import jax
import jax.numpy as jnp
from jax import lax

D = 8192
HQ = 64
KVH = 8
HD = 128
VOCAB = 65536
NODES = 64
PATH = 6
BATCH = 2
CTX_DEV = 1024
CTX = 8192
N_SEQ = 8


def tree_shape(key):
    source = jax.random.fold_in(key, 101)
    node_ids = jnp.arange(NODES, dtype=jnp.int32)
    upper = jnp.maximum(node_ids, 1)
    parents = jax.random.randint(jax.random.fold_in(source, 1), (BATCH, NODES), 0, upper[None, :], dtype=jnp.int32)
    row_keys = jax.random.split(jax.random.fold_in(source, 2), BATCH)
    short_keys = jax.random.split(jax.random.fold_in(source, 3), BATCH)

    def shuffle(row_key):
        return jax.random.permutation(row_key, NODES - 1).astype(jnp.int32) + 1

    def shuffle_short(row_key):
        return jax.random.permutation(row_key, NODES - 3).astype(jnp.int32) + 1
    orders = jax.vmap(shuffle)(row_keys)
    chosen_free = jnp.sort(orders[:, :PATH - 1], axis=1)
    short_orders = jax.vmap(shuffle_short)(short_keys)
    head_part = jnp.sort(short_orders[:, :PATH - 3], axis=1)
    tail_part = jnp.broadcast_to(jnp.array([NODES - 2, NODES - 1], dtype=jnp.int32)[None, :], (BATCH, 2))
    chosen_end = jnp.concatenate([head_part, tail_part], axis=1)
    special = jax.random.randint(jax.random.fold_in(source, 4), (), 0, BATCH, dtype=jnp.int32)
    is_special = (jnp.arange(BATCH, dtype=jnp.int32) == special)[:, None]
    chosen = jnp.where(is_special, chosen_end, chosen_free)
    path = jnp.concatenate([jnp.zeros((BATCH, 1), jnp.int32), chosen], axis=1)
    hits = node_ids[None, None, :] == path[:, 1:, None]
    forced = jnp.sum(jnp.where(hits, path[:, :-1, None], 0), axis=1)
    parents = jnp.where(jnp.any(hits, axis=1), forced, parents)
    return (parents.astype(jnp.int32), path.astype(jnp.int32))


def draw_parents(key, part):
    return tree_shape(key)[0]


def draw_path(key, part):
    return tree_shape(key)[1]


def fresh_keys(key):
    source = jax.random.fold_in(key, 202)
    shape = (BATCH, KVH, NODES, HD)
    raw = 5.0 * jax.random.truncated_normal(jax.random.fold_in(source, 1), -3.8, 3.8, shape, jnp.float32)
    return raw


def draw_new_keys(key, part):
    return fresh_keys(key).astype(jnp.bfloat16)


def draw_queries(key, part):
    source = jax.random.fold_in(key, 303)
    shape = (BATCH, HQ, NODES, HD)
    raw = 1.7 * jax.random.truncated_normal(jax.random.fold_in(source, 1), -4.5, 4.5, shape, jnp.float32)
    return raw.astype(jnp.bfloat16)


def draw_cache_keys(key, part):
    source = jax.random.fold_in(key, 707)
    shape = (BATCH, KVH, CTX, HD)
    raw = 1.7 * jax.random.truncated_normal(jax.random.fold_in(source, 1), -10.0 / 1.7, 10.0 / 1.7, shape, jnp.float32)
    return raw.astype(jnp.bfloat16)


def draw_lengths(key, part):
    raw = jax.random.randint(jax.random.fold_in(key, 505), (BATCH,), CTX // 4, CTX + 1, dtype=jnp.int32)
    filled = jax.random.randint(jax.random.fold_in(key, 506), (), 0, BATCH, dtype=jnp.int32)
    return jnp.where(jnp.arange(BATCH, dtype=jnp.int32) == filled, CTX, raw).astype(jnp.int32)


def draw_residual(key, part):
    source = jax.random.fold_in(key, 606)
    columns = jnp.arange(D, dtype=jnp.float32) / D
    rising = 0.15 * jnp.exp(jnp.log(3.0) * columns)
    jitter = jnp.exp(jax.random.uniform(jax.random.fold_in(source, 1), (D,), jnp.float32, -0.69, 0.69))
    raw = jax.random.truncated_normal(jax.random.fold_in(source, 2), -5.0, 5.0, (BATCH, NODES, D), jnp.float32)
    return (raw * rising * jitter).astype(jnp.bfloat16)


def draw_vocab_weight(key, part):
    source = jax.random.fold_in(key, 404)
    spread = 3.0 / jnp.sqrt(jnp.float32(D))
    raw = spread * jax.random.truncated_normal(jax.random.fold_in(source, 1), -5.0, 5.0, (D, VOCAB), jnp.float32)
    return raw.astype(jnp.bfloat16)


def touch_ends(values, key, smallest, top_value):
    dims = values.shape
    place = [jax.random.randint(jax.random.fold_in(key, axis), (), 0, dims[axis]) for axis in range(len(dims))]
    values = values.at[tuple(place)].set(smallest)
    longest = dims.index(max(dims))
    place[longest] = (place[longest] + 1) % dims[longest]
    return values.at[tuple(place)].set(top_value)


def steps_of(stream_key, shape, pieces, smallest, top_value):
    def one(axis_at, parts):
        draws = jax.random.uniform(jax.random.fold_in(jax.random.fold_in(stream_key, 6), axis_at), (parts,), jnp.float32, smallest / len(pieces), top_value / len(pieces))
        return jnp.repeat(jnp.exp(draws), shape[axis_at] // parts).reshape((-1,) + (1,) * (len(shape) - axis_at - 1))

    factor_of = one(*pieces[0])
    for cut in pieces[1:]:
        factor_of = factor_of * one(*cut)
    return factor_of


def bell_draw(rng, dims, width, most, cuts=(), kind=jnp.bfloat16):
    factor_of = steps_of(rng, dims, cuts, -0.22, 0.18) if cuts else 1.0
    values = jax.random.normal(rng, dims, jnp.float32) * width * factor_of
    return jnp.minimum(jnp.maximum(values, -most), most).astype(kind)


def setup_inputs(seed: int = 0) -> dict:
    arg_keys = jax.random.split(jax.random.key(seed), 14)
    queries = draw_queries(jax.random.fold_in(arg_keys[13], 71), 0)
    cache_keys = draw_cache_keys(jax.random.fold_in(arg_keys[13], 71), 0)
    cache_values = bell_draw(arg_keys[2], (BATCH, KVH, CTX, HD), 1.0, 6.0, ((1, 4), (2, 8)))
    new_keys = draw_new_keys(jax.random.fold_in(arg_keys[13], 71), 0)
    new_values = bell_draw(arg_keys[4], (BATCH, KVH, NODES, HD), 1.0, 6.0, ((1, 4),))
    parents = draw_parents(jax.random.fold_in(arg_keys[13], 71), 0)
    path = draw_path(jax.random.fold_in(arg_keys[13], 71), 0)
    lengths = draw_lengths(jax.random.fold_in(arg_keys[13], 71), 0)
    draft_tokens = touch_ends(jax.random.randint(arg_keys[8], (BATCH, NODES), 0, VOCAB), jax.random.fold_in(arg_keys[8], 1), 0, VOCAB - 1).astype(jnp.int32)
    residual = draw_residual(jax.random.fold_in(arg_keys[13], 71), 0)
    out_weight = bell_draw(arg_keys[10], (HQ * HD, D), (HQ * HD) ** -0.5, 0.0625, ((0, 4), (1, 8)))
    norm_gain = jnp.clip(1.0 + 0.1 * jax.random.normal(arg_keys[11], (D,), jnp.float32), 0.5, 1.5).astype(jnp.bfloat16)
    vocab_weight = draw_vocab_weight(jax.random.fold_in(arg_keys[13], 71), 0)
    return {"queries": queries, "cache_keys": cache_keys, "cache_values": cache_values, "new_keys": new_keys, "new_values": new_values, "parents": parents, "path": path, "lengths": lengths, "draft_tokens": draft_tokens, "residual": residual, "out_weight": out_weight, "norm_gain": norm_gain, "vocab_weight": vocab_weight}


lowest = -1e+30
epsilon = 1e-05

def ancestors(parents):
    node_count = parents.shape[-1]
    node_ids = jnp.arange(node_count, dtype=jnp.int32)
    linked = (parents[..., :, None] == node_ids[None, None, :]).astype(jnp.float32)
    reached = jnp.maximum(linked, jnp.eye(node_count, dtype=jnp.float32)[None])
    for _ in range(node_count.bit_length()):
        reached = jnp.minimum(jnp.einsum('bij,bjk->bik', reached, reached), 1.0)
    return reached > 0.5

def block_state(scores, visible, values):
    masked = jnp.where(visible, scores, lowest)
    block_max = lax.optimization_barrier(jnp.max(masked, axis=-1))
    weights = jnp.where(visible, jnp.exp(masked - block_max[..., None]), 0.0).astype(jnp.bfloat16)
    block_total = lax.optimization_barrier(jnp.sum(weights.astype(jnp.float32), axis=-1))
    block_out = jnp.einsum('kqc,kcd->kqd', weights.astype(jnp.float32), values.astype(jnp.float32))
    return (block_max, block_total, block_out)

def reference(queries, cache_keys, cache_values, new_keys, new_values, parents, path, lengths, draft_tokens, residual, out_weight, norm_gain, vocab_weight):
    group_size = HQ // KVH
    score_scale = HD ** (-0.5)
    reached = ancestors(parents)
    positions = jnp.arange(CTX_DEV, dtype=jnp.int32)

    def per_sequence(entries):
        query_block, key_block, value_block, tree_keys, tree_values, reach_row, length = entries
        grouped = query_block.reshape(KVH, group_size * NODES, HD).astype(jnp.float32)
        tree_scores = jnp.einsum('kqd,kcd->kqc', grouped, tree_keys.astype(jnp.float32)) * score_scale
        tree_seen = jnp.tile(reach_row, (group_size, 1))[None]
        tree_max, tree_total, tree_out = block_state(tree_scores, tree_seen, tree_values)

        def per_block(anchor):
            block_keys = lax.dynamic_slice_in_dim(key_block, anchor, CTX_DEV, 1)
            block_values = lax.dynamic_slice_in_dim(value_block, anchor, CTX_DEV, 1)
            scores = jnp.einsum('kqd,kcd->kqc', grouped, block_keys.astype(jnp.float32)) * score_scale
            live_keys = (anchor + positions < length)[None, None, :]
            return block_state(scores, live_keys, block_values)
        anchors = jnp.arange(N_SEQ, dtype=jnp.int32) * CTX_DEV
        maxima, totals, outputs = lax.map(per_block, anchors)
        maxima = jnp.concatenate([maxima, tree_max[None]], 0)
        totals = jnp.concatenate([totals, tree_total[None]], 0)
        outputs = jnp.concatenate([outputs, tree_out[None]], 0)
        highest = lax.optimization_barrier(jnp.max(maxima, axis=0))
        factors = jnp.exp(maxima - highest[None])
        whole_total = lax.optimization_barrier(jnp.sum(totals * factors, axis=0))
        whole_out = lax.optimization_barrier(jnp.sum(outputs * factors[..., None], axis=0))
        result = (whole_out / whole_total[..., None]).astype(jnp.bfloat16)
        return result.reshape(HQ, NODES, HD)
    attention = lax.map(per_sequence, (queries, cache_keys, cache_values, new_keys, new_values, reached, lengths))
    projected = jnp.einsum('bhnd,hdc->bnc', attention.astype(jnp.float32), out_weight.reshape(HQ, HD, D).astype(jnp.float32))
    stream = residual.astype(jnp.float32) + projected
    mean_square = lax.optimization_barrier(jnp.sum(stream * stream, axis=-1)) / D
    normed = (stream * lax.rsqrt(mean_square + epsilon)[..., None] * norm_gain.astype(jnp.float32)).astype(jnp.bfloat16)
    flat_rows = normed.reshape(BATCH * NODES, D).astype(jnp.float32)
    block_width = VOCAB // 8

    def vocab_block(anchor):
        columns = lax.dynamic_slice_in_dim(vocab_weight, anchor, block_width, 1).astype(jnp.float32)
        return jnp.dot(flat_rows, columns, precision=lax.Precision.HIGHEST)
    blocks = lax.map(vocab_block, jnp.arange(8, dtype=jnp.int32) * block_width)
    logits = jnp.transpose(blocks, (1, 0, 2)).reshape(BATCH, NODES, VOCAB)
    path_logits = jnp.take_along_axis(logits, path[:, :, None], axis=1)
    vocab_top = lax.optimization_barrier(jnp.max(logits, axis=-1))
    vocab_sum = lax.optimization_barrier(jnp.sum(jnp.exp(logits - vocab_top[..., None]), axis=-1))
    picked = jnp.take_along_axis(logits, draft_tokens[:, :, None], axis=2)[..., 0]
    draft_logprob = picked - (vocab_top + jnp.log(vocab_sum))
    return (path_logits, draft_logprob)
```

```python
import functools
import math

import jax
import jax.numpy as jnp
from jax import lax
from jax.experimental import pallas as pl
from jax.experimental.pallas import tpu as pltpu
from jax.sharding import PartitionSpec as P

lowest = -1e30
epsilon = 1e-05
MESH = pl.DeviceIdType.MESH
f32 = jnp.float32
bf16 = jnp.bfloat16


def kernel(
    S, H, B, N, D,
    len_ref, path_ref, par_ref, draft_ref, gain_ref,
    q_hbm, k_hbm, v_hbm, nk_hbm, nv_hbm, res_hbm, ow_hbm, vw_hbm,
    path_out, logp_out,
    q, k, v, res, ow, vw, reach,
    o_send, ml_send, o_recv, ml_recv, a_send, x_att, p_send, p_recv, g, acc,
    ss_send, ss_r1, ss_mid, ss_r2, st_send, st_r1, st_mid, st_r2,
    load_sem, vw_sem,
    o_ss, o_rs, ml_ss, ml_rs, a_ss, a_rs, p_ss, p_rs, g_ss, g_rs,
    s1_ss, s1_rs, s2_ss, s2_rs, t1_ss, t1_rs, t2_ss, t2_rs,
):
    s = lax.axis_index("seq")
    h = lax.axis_index("head")
    R, HD = q.shape[1], q.shape[2]
    BK, keys = k.shape[0], k_hbm.shape[1]
    parts = S // BK
    rows = B * N
    HR = rows // H
    DL = ow.shape[1]
    VL = vw.shape[1]
    heads_chunk = R // N
    group = S // B

    def seq_peer(i):
        return lax.rem(s + i, S)

    def head_peer(i):
        return lax.rem(h + i, H)

    loads = [
        (q_hbm, q),
        (k_hbm, k.at[:, pl.ds(0, keys)]),
        (nk_hbm, k.at[:, pl.ds(keys, N)]),
        (v_hbm, v.at[:, pl.ds(0, keys)]),
        (nv_hbm, v.at[:, pl.ds(keys, N)]),
        (res_hbm, res),
        (ow_hbm, ow),
    ]
    loads = [
        pltpu.make_async_copy(src, dst, load_sem.at[i]) for i, (src, dst) in enumerate(loads)
    ]
    for c in loads:
        c.start()

    barrier = pltpu.get_barrier_semaphore()
    for i in range(1, S):
        pl.semaphore_signal(barrier, inc=1, device_id=(seq_peer(i), h), device_id_type=MESH)
    for i in range(1, H):
        pl.semaphore_signal(barrier, inc=1, device_id=(s, head_peer(i)), device_id_type=MESH)

    Z = S // 2
    y = lax.rem(s, 2)
    z = s // 2
    order = []
    for i in range(Z):
        zi = lax.rem(z + i, Z)
        order.append(zi * 2 + y)
        order.append(zi * 2 + (1 - y))

    def slab(idx):
        return pl.ds(pl.multiple_of(idx * DL, DL), DL)

    def vw_copy(n):
        return pltpu.make_async_copy(
            vw_hbm.at[slab(order[n])], vw.at[slab(order[n])], vw_sem.at[n]
        )

    for n in range(S):
        vw_copy(n).start()

    rid = lax.broadcasted_iota(jnp.int32, (N, N), 0)
    cid = lax.broadcasted_iota(jnp.int32, (N, N), 1)
    for b in range(B):
        link = jnp.logical_or(par_ref[b : b + 1, :] == rid, rid == cid)
        r = jnp.where(link, 1.0, 0.0)
        for _ in range(N.bit_length() - 1):
            rb = r.astype(bf16)
            r = jnp.minimum(jnp.dot(rb, rb, preferred_element_type=f32), 1.0)
        reach[b] = jnp.concatenate([r] * heads_chunk, axis=1)

    for c in loads[:5]:
        c.wait()

    scale = math.log2(math.e) * HD**-0.5
    key_id = lax.broadcasted_iota(jnp.int32, (keys, R), 0) + s * keys
    owner = s == 0

    def chunk(t):
        bk = t // parts
        b = t // group
        kk = k[bk]
        vv = v[bk]
        length = len_ref[0]
        for i in range(1, B):
            length = jnp.where(b == i, len_ref[i], length)
        score = lax.dot_general(kk, q[t], (((1,), (1,)), ((), ())), preferred_element_type=f32)
        cache = jnp.where(key_id < length, score[:keys] * scale, lowest)
        tree_seen = jnp.where(owner, reach[b], 0.0) > 0.5
        tree = jnp.where(tree_seen, score[keys:] * scale, lowest)
        top = jnp.maximum(
            jnp.max(cache, axis=0, keepdims=True), jnp.max(tree, axis=0, keepdims=True)
        )
        top = jnp.maximum(top, 0.1 * lowest)
        wc = jnp.exp2(cache - top)
        wt = jnp.exp2(tree - top)
        total = jnp.sum(wc, axis=0, keepdims=True) + jnp.sum(wt, axis=0, keepdims=True)
        w = jnp.concatenate([wc.astype(bf16), wt.astype(bf16)], axis=0)
        out = lax.dot_general(vv, w, (((0,), (0,)), ((), ())), preferred_element_type=f32)
        ml = jnp.concatenate(
            [jnp.broadcast_to(top, (4, R)), jnp.broadcast_to(total, (4, R))], axis=0
        )
        return out.astype(bf16), ml

    def remote(src, dst, ss, rs, dev):
        return pltpu.make_async_remote_copy(
            src_ref=src, dst_ref=dst, send_sem=ss, recv_sem=rs, device_id=dev, device_id_type=MESH
        )

    pl.semaphore_wait(barrier, S - 1 + H - 1)

    def send_chunk(i, carry):
        t = seq_peer(i)
        out, ml = chunk(t)
        o_send[t] = out
        ml_send[t] = ml
        remote(o_send.at[t], o_recv.at[s], o_ss.at[t], o_rs.at[s], (t, h)).start()
        remote(ml_send.at[t], ml_recv.at[s], ml_ss.at[t], ml_rs.at[s], (t, h)).start()
        return carry

    lax.fori_loop(1, S, send_chunk, 0)
    out, ml = chunk(s)
    o_recv[s] = out
    ml_recv[s] = ml

    for i in range(1, S):
        t = seq_peer(i)
        remote(o_send.at[t], o_recv.at[t], o_ss.at[t], o_rs.at[t], (t, h)).wait_recv()
        remote(ml_send.at[t], ml_recv.at[t], ml_ss.at[t], ml_rs.at[t], (t, h)).wait_recv()

    top = ml_recv[0, 0:1]
    for i in range(1, S):
        top = jnp.maximum(top, ml_recv[i, 0:1])
    total = jnp.zeros((1, R), f32)
    whole = jnp.zeros((HD, R), f32)
    for i in range(S):
        w = jnp.exp2(ml_recv[i, 0:1] - top)
        total += ml_recv[i, 4:5] * w
        whole += o_recv[i].astype(f32) * w
    att = jnp.transpose(whole / total).astype(bf16).reshape(heads_chunk, N, HD)

    def att_place(t):
        h0 = lax.rem(t, group) * heads_chunk
        return x_att.at[pl.ds(h0, heads_chunk), pl.ds(pl.multiple_of(t // group * N, N), N), :]

    a_send[...] = att
    for i in range(1, S):
        t = seq_peer(i)
        remote(a_send, att_place(s), a_ss.at[t], a_rs.at[s], (t, h)).start()
    x_att[
        pl.ds(lax.rem(s, group) * heads_chunk, heads_chunk),
        pl.ds(pl.multiple_of(s // group * N, N), N),
        :,
    ] = att
    loads[5].wait()
    loads[6].wait()
    for i in range(1, S):
        t = seq_peer(i)
        remote(a_send, att_place(t), a_ss.at[t], a_rs.at[t], (t, h)).wait_recv()

    lhs = jnp.concatenate([x_att[i] for i in range(x_att.shape[0])], axis=1)
    proj = jnp.dot(lhs, ow[...], preferred_element_type=f32)
    for j in range(H):
        p_send[j] = proj[j * HR : (j + 1) * HR].astype(bf16)
    for i in range(1, H):
        t = head_peer(i)
        remote(p_send.at[t], p_recv.at[h], p_ss.at[t], p_rs.at[h], (s, t)).start()
    my_rows = pl.ds(pl.multiple_of(h * HR, HR), HR)
    stream = res[my_rows, :].astype(f32) + p_send[h].astype(f32)
    for i in range(1, H):
        t = head_peer(i)
        remote(p_send.at[t], p_recv.at[t], p_ss.at[t], p_rs.at[t], (s, t)).wait_recv()
        stream += p_recv[t].astype(f32)
    g[s, my_rows, :] = (stream * gain_ref[...].astype(f32)).astype(bf16)

    def block(si, hi):
        return g.at[si, pl.ds(pl.multiple_of(hi * HR, HR), HR), :]

    sends = []

    def pass_on(si, hi, dev):
        c = remote(block(si, hi), block(si, hi), g_ss.at[len(sends)], g_rs.at[si * H + hi], dev)
        c.start()
        sends.append(c)

    def arrive(si, hi):
        remote(block(si, hi), block(si, hi), g_ss.at[0], g_rs.at[si * H + hi], (s, h)).wait_recv()

    HX = H // 2
    hx, hc = h // 2, lax.rem(h, 2)
    partner = hx * 2 + (1 - hc)
    far = [lax.rem(hx + i, HX) * 2 + hc for i in range(1, HX)]
    far_partner = [lax.rem(hx + i, HX) * 2 + (1 - hc) for i in range(1, HX)]
    y_dev = z * 2 + (1 - y)

    def first_hop(n):
        si = order[n]
        if n == 0:
            for i in range(1, Z):
                pass_on(si, h, (order[2 * i], h))
        else:
            arrive(si, h)
        if n % 2 == 0:
            pass_on(si, h, (y_dev, h))
        for t in far:
            pass_on(si, h, (s, t))
        pass_on(si, h, (s, partner))

    def second_hop(n):
        for t in far:
            arrive(order[n], t)
            pass_on(order[n], t, (s, partner))

    tiles = max(1, VL // 512)
    width = VL // tiles

    def product(n):
        arrive(order[n], partner)
        for t in far_partner:
            arrive(order[n], t)
        vw_copy(n).wait()
        left = g[order[n]]

        def tile(c, carry):
            cols = pl.ds(pl.multiple_of(c * width, width), width)
            part = jnp.dot(left, vw[slab(order[n]), cols], preferred_element_type=f32)
            acc[:, cols] = part if n == 0 else acc[:, cols] + part
            return carry

        lax.fori_loop(0, tiles, tile, 0)

    first_hop(0)

    eye = lax.broadcasted_iota(jnp.int32, (rows, rows), 0) == lax.broadcasted_iota(
        jnp.int32, (rows, rows), 1
    )

    def to_row(col):
        return jnp.sum(jnp.where(eye, col, 0.0), axis=0, keepdims=True)

    def to_col(row):
        return jnp.sum(jnp.where(eye, row, 0.0), axis=1, keepdims=True)

    squares = jnp.sum(stream * stream, axis=1, keepdims=True)
    mine = lax.broadcasted_iota(jnp.int32, (HR, rows), 0) + h * HR == lax.broadcasted_iota(
        jnp.int32, (HR, rows), 1
    )
    square_row = jnp.sum(jnp.where(mine, squares, 0.0), axis=0, keepdims=True)
    ss_send[...] = jnp.broadcast_to(square_row, (8, rows))
    for i in range(1, S):
        t = seq_peer(i)
        remote(ss_send, ss_r1.at[s], s1_ss.at[t], s1_rs.at[s], (t, h)).start()
    ss_r1[s] = ss_send[...]

    def squares_on():
        for i in range(1, S):
            t = seq_peer(i)
            remote(ss_send, ss_r1.at[t], s1_ss.at[t], s1_rs.at[t], (t, h)).wait_recv()
        part = ss_r1[0]
        for i in range(1, S):
            part = part + ss_r1[i]
        ss_mid[...] = part
        ss_r2[h] = part
        for i in range(1, H):
            t = head_peer(i)
            remote(ss_mid, ss_r2.at[h], s2_ss.at[t], s2_rs.at[h], (s, t)).start()

    for n in range(S + 2):
        if n + 1 < S:
            first_hop(n + 1)
        if n == 2:
            squares_on()
        if n < S:
            second_hop(n)
        if n >= 1 and n - 1 < S:
            product(n - 1)

    for i in range(1, H):
        t = head_peer(i)
        remote(ss_mid, ss_r2.at[t], s2_ss.at[t], s2_rs.at[t], (s, t)).wait_recv()
    square_sum = ss_r2[0, 0:1]
    for i in range(1, H):
        square_sum = square_sum + ss_r2[i, 0:1]
    inverse = to_col(lax.rsqrt(square_sum / D + epsilon))
    logits = acc[...] * inverse
    acc[...] = logits
    local_top = jnp.max(logits, axis=1, keepdims=True)
    local_sum = jnp.sum(jnp.exp(logits - local_top), axis=1, keepdims=True)
    ids = lax.broadcasted_iota(jnp.int32, (rows, VL), 1) + (s * H + h) * VL
    wanted = to_col(draft_ref[...].astype(f32)).astype(jnp.int32)
    picked = jnp.sum(jnp.where(ids == wanted, logits, 0.0), axis=1, keepdims=True)
    stat = [to_row(local_top), to_row(local_sum), to_row(picked)]

    def pack(stat):
        return jnp.concatenate(stat + [jnp.zeros((5, rows), f32)], axis=0)

    def merge(ref, count):
        top = ref[0, 0:1]
        for i in range(1, count):
            top = jnp.maximum(top, ref[i, 0:1])
        total = jnp.zeros((1, rows), f32)
        got = jnp.zeros((1, rows), f32)
        for i in range(count):
            total += ref[i, 1:2] * jnp.exp(ref[i, 0:1] - top)
            got += ref[i, 2:3]
        return [top, total, got]

    st_send[...] = pack(stat)
    for i in range(1, S):
        t = seq_peer(i)
        remote(st_send, st_r1.at[s], t1_ss.at[t], t1_rs.at[s], (t, h)).start()
    st_r1[s] = pack(stat)
    for b in range(B):
        for i in range(path_ref.shape[1]):
            path_out[b, i : i + 1, :] = acc[pl.ds(path_ref[b, i] + b * N, 1), :]
    for i in range(1, S):
        t = seq_peer(i)
        remote(st_send, st_r1.at[t], t1_ss.at[t], t1_rs.at[t], (t, h)).wait_recv()
    both = pack(merge(st_r1, S))
    st_mid[...] = both
    st_r2[h] = both
    for i in range(1, H):
        t = head_peer(i)
        remote(st_mid, st_r2.at[h], t2_ss.at[t], t2_rs.at[h], (s, t)).start()
    for i in range(1, H):
        t = head_peer(i)
        remote(st_mid, st_r2.at[t], t2_ss.at[t], t2_rs.at[t], (s, t)).wait_recv()
    top, total, got = merge(st_r2, H)
    logp_out[...] = got - (top + jnp.log(total))

    for i in range(1, S):
        t = seq_peer(i)
        remote(o_send.at[t], o_recv.at[s], o_ss.at[t], o_rs.at[s], (t, h)).wait_send()
        remote(ml_send.at[t], ml_recv.at[s], ml_ss.at[t], ml_rs.at[s], (t, h)).wait_send()
        remote(a_send, att_place(s), a_ss.at[t], a_rs.at[s], (t, h)).wait_send()
        remote(ss_send, ss_r1.at[s], s1_ss.at[t], s1_rs.at[s], (t, h)).wait_send()
        remote(st_send, st_r1.at[s], t1_ss.at[t], t1_rs.at[s], (t, h)).wait_send()
    for i in range(1, H):
        t = head_peer(i)
        remote(p_send.at[t], p_recv.at[h], p_ss.at[t], p_rs.at[h], (s, t)).wait_send()
        remote(ss_mid, ss_r2.at[h], s2_ss.at[t], s2_rs.at[h], (s, t)).wait_send()
        remote(st_mid, st_r2.at[h], t2_ss.at[t], t2_rs.at[h], (s, t)).wait_send()
    for c in sends:
        c.wait_send()


def on_device(
    S,
    H,
    queries,
    cache_keys,
    cache_values,
    new_keys,
    new_values,
    parents,
    path,
    lengths,
    draft_tokens,
    residual,
    out_weight,
    norm_gain,
    vocab_weight,
):
    B, heads, N, HD = queries.shape
    KV, keys = cache_keys.shape[1], cache_keys.shape[2]
    BK = B * KV
    R = B * heads * N // S
    rows = B * N
    DL = out_weight.shape[1]
    D, VL = vocab_weight.shape
    K = out_weight.shape[0]
    HR = rows // H
    HX = H // 2
    passes = (S // 2 - 1) + S // 2 + S * (HX - 1) + S + S * (HX - 1)
    vmem = pl.BlockSpec(memory_space=pltpu.VMEM)
    smem = pl.BlockSpec(memory_space=pltpu.SMEM)
    hbm = pl.BlockSpec(memory_space=pl.ANY)
    dma = pltpu.SemaphoreType.DMA
    path_logits, logp = pl.pallas_call(
        functools.partial(kernel, S, H, B, N, D),
        out_shape=(
            jax.ShapeDtypeStruct((B, path.shape[1], VL), f32),
            jax.ShapeDtypeStruct((1, rows), f32),
        ),
        in_specs=[smem, smem, vmem, vmem, vmem] + [hbm] * 8,
        out_specs=(vmem, vmem),
        scratch_shapes=[
            pltpu.VMEM((S, R, HD), bf16),
            pltpu.VMEM((BK, keys + N, HD), bf16),
            pltpu.VMEM((BK, keys + N, HD), bf16),
            pltpu.VMEM((rows, DL), bf16),
            pltpu.VMEM((K, DL), bf16),
            pltpu.VMEM((D, VL), bf16),
            pltpu.VMEM((B, N, R), f32),
            pltpu.VMEM((S, HD, R), bf16),
            pltpu.VMEM((S, 8, R), f32),
            pltpu.VMEM((S, HD, R), bf16),
            pltpu.VMEM((S, 8, R), f32),
            pltpu.VMEM((R // N, N, HD), bf16),
            pltpu.VMEM((heads, rows, HD), bf16),
            pltpu.VMEM((H, HR, DL), bf16),
            pltpu.VMEM((H, HR, DL), bf16),
            pltpu.VMEM((S, rows, DL), bf16),
            pltpu.VMEM((rows, VL), f32),
            pltpu.VMEM((8, rows), f32),
            pltpu.VMEM((S, 8, rows), f32),
            pltpu.VMEM((8, rows), f32),
            pltpu.VMEM((H, 8, rows), f32),
            pltpu.VMEM((8, rows), f32),
            pltpu.VMEM((S, 8, rows), f32),
            pltpu.VMEM((8, rows), f32),
            pltpu.VMEM((H, 8, rows), f32),
            dma((7,)),
            dma((S,)),
            dma((S,)), dma((S,)), dma((S,)), dma((S,)), dma((S,)), dma((S,)),
            dma((H,)), dma((H,)),
            dma((passes,)), dma((S * H,)),
            dma((S,)), dma((S,)), dma((H,)), dma((H,)),
            dma((S,)), dma((S,)), dma((H,)), dma((H,)),
        ],
        compiler_params=pltpu.CompilerParams(
            collective_id=0, has_side_effects=True, vmem_limit_bytes=62 * 1024 * 1024
        ),
        name="verify",
    )(
        lengths,
        path,
        parents,
        draft_tokens.reshape(1, rows),
        norm_gain.reshape(1, DL),
        queries.reshape(S, R, HD),
        cache_keys.reshape(BK, keys, HD),
        cache_values.reshape(BK, keys, HD),
        new_keys.reshape(BK, N, HD),
        new_values.reshape(BK, N, HD),
        residual.reshape(rows, DL),
        out_weight,
        vocab_weight,
    )
    return path_logits, logp.reshape(B, N)


def solution(mesh):
    placed = (
        P(None, "head", None, None),
        P(None, "head", "seq", None),
        P(None, "head", "seq", None),
        P(None, "head", None, None),
        P(None, "head", None, None),
        P(),
        P(),
        P(),
        P(),
        P(None, None, "seq"),
        P("head", "seq"),
        P("seq"),
        P(None, ("seq", "head")),
    )
    return jax.shard_map(
        functools.partial(on_device, mesh.shape["seq"], mesh.shape["head"]),
        mesh=mesh,
        in_specs=placed,
        out_specs=(P(None, None, ("seq", "head")), P()),
        check_vma=False,
    )
```

```python
import functools
import math

import jax
import jax.numpy as jnp
from jax import lax
from jax.experimental import pallas as pl
from jax.experimental.pallas import tpu as pltpu
from jax.sharding import PartitionSpec as P

lowest = -1e30
epsilon = 1e-05
MESH = pl.DeviceIdType.MESH
f32 = jnp.float32
bf16 = jnp.bfloat16


def route_steps(S, H):
    names = []
    for kind, count in (("z", S // 2), ("y", 2), ("x", H // 2), ("c", 2)):
        while count > 1:
            names.append((kind, count))
            count //= 2
    return names


def subsets(names):
    out = [frozenset()]
    for n in names:
        out += [c | {n} for c in out]
    return out


def last_step(offset, names):
    return [n for n in names if n in offset][-1]


def balanced(offset):
    parts = {kind: sorted([n for n in offset if n[0] == kind], reverse=True) for kind in "zyxc"}
    if parts["c"]:
        return parts["c"][-1]
    if parts["x"] and parts["y"]:
        return parts["x"][-1] if len(parts["z"]) > 1 else parts["y"][-1]
    if parts["x"]:
        return parts["x"][-1]
    if parts["y"]:
        return parts["z"][-1] if len(parts["z"]) == 1 else parts["y"][-1]
    return parts["z"][-1]


def plan(names, via):
    price = {n: 0.9 if n[0] == "c" else 1.6 + 0.75 * (min(n[1], 4) - 2) for n in names}
    every = subsets(names)
    cost = {frozenset(): 0.0}
    for c in sorted(every, key=len):
        if c:
            n = via(c)
            cost[c] = cost[c - {n}] + price[n] + 0.7
    onward = {c: [n for n in names if n not in c and via(c | {n}) == n] for c in every}
    rank = sorted(every, key=lambda c: (cost[c], sorted(c)))
    return [(c, cost[c], onward[c]) for c in rank]


def kernel(
    S, H, B, N, D,
    len_ref, path_ref, par_ref, draft_ref, gain_ref,
    q_hbm, k_hbm, v_hbm, nk_hbm, nv_hbm, res_hbm, ow_hbm, vw_hbm,
    path_out, logp_out,
    q, k, v, res, ow, vw, reach,
    o_send, ml_send, o_recv, ml_recv, a_send, x_att, p_send, p_recv, g, acc,
    ss_send, ss_r1, ss_mid, ss_r2, st_send, st_r1, st_mid, st_r2,
    load_sem, vw_sem,
    o_ss, o_rs, ml_ss, ml_rs, a_ss, a_rs, p_ss, p_rs, g_ss, g_rs,
    s1_ss, s1_rs, s2_ss, s2_rs, t1_ss, t1_rs, t2_ss, t2_rs,
):
    s = lax.axis_index("seq")
    h = lax.axis_index("head")
    R, HD = q.shape[1], q.shape[2]
    BK, keys = k.shape[0], k_hbm.shape[1]
    parts = S // BK
    rows = B * N
    HR = rows // H
    DL = ow.shape[1]
    VL = vw.shape[1]
    heads_chunk = R // N
    group = S // B

    def seq_peer(i):
        return lax.rem(s + i, S)

    def head_peer(i):
        return lax.rem(h + i, H)

    loads = [
        (q_hbm, q),
        (k_hbm, k.at[:, pl.ds(0, keys)]),
        (nk_hbm, k.at[:, pl.ds(keys, N)]),
        (v_hbm, v.at[:, pl.ds(0, keys)]),
        (nv_hbm, v.at[:, pl.ds(keys, N)]),
        (res_hbm, res),
        (ow_hbm, ow),
    ]
    loads = [
        pltpu.make_async_copy(src, dst, load_sem.at[i]) for i, (src, dst) in enumerate(loads)
    ]
    for c in loads:
        c.start()

    barrier = pltpu.get_barrier_semaphore()
    for i in range(1, S):
        pl.semaphore_signal(barrier, inc=1, device_id=(seq_peer(i), h), device_id_type=MESH)
    for i in range(1, H):
        pl.semaphore_signal(barrier, inc=1, device_id=(s, head_peer(i)), device_id_type=MESH)

    steps = route_steps(S, H)

    def flip(value, span):
        return 2 * (value // span * span) + span - 1 - value

    def at_offset(offset):
        zi, yi, xi, ci = s // 2, lax.rem(s, 2), h // 2, lax.rem(h, 2)
        for name in offset:
            kind, span = name
            if kind == "z":
                zi = flip(zi, span)
            elif kind == "y":
                yi = 1 - yi
            elif kind == "x":
                xi = flip(xi, span)
            else:
                ci = 1 - ci
        return zi * 2 + yi, xi * 2 + ci

    zy = [n for n in steps if n[0] in "zy"]
    row_plan = plan(steps, balanced)
    att_plan = plan(zy, lambda c: last_step(c, zy))
    row_cost = {c: cost for c, cost, _ in row_plan}
    xc = subsets([n for n in steps if n[0] in "xc"])
    slabs = sorted(subsets(zy), key=lambda c: (max(row_cost[c | o] for o in xc), sorted(c)))
    order = [at_offset(c)[0] for c in slabs]

    def slab(idx):
        return pl.ds(pl.multiple_of(idx * DL, DL), DL)

    def vw_copy(n):
        return pltpu.make_async_copy(
            vw_hbm.at[slab(order[n])], vw.at[slab(order[n])], vw_sem.at[n]
        )

    for n in range(S):
        vw_copy(n).start()

    rid = lax.broadcasted_iota(jnp.int32, (N, N), 0)
    cid = lax.broadcasted_iota(jnp.int32, (N, N), 1)
    for b in range(B):
        link = jnp.logical_or(par_ref[b : b + 1, :] == rid, rid == cid)
        r = jnp.where(link, 1.0, 0.0)
        for _ in range(N.bit_length() - 1):
            rb = r.astype(bf16)
            r = jnp.minimum(jnp.dot(rb, rb, preferred_element_type=f32), 1.0)
        reach[b] = jnp.concatenate([r] * heads_chunk, axis=1)

    for c in loads[:5]:
        c.wait()

    scale = math.log2(math.e) * HD**-0.5
    key_id = lax.broadcasted_iota(jnp.int32, (keys, R), 0) + s * keys
    owner = s == 0

    def chunk(t):
        bk = t // parts
        b = t // group
        kk = k[bk]
        vv = v[bk]
        length = len_ref[0]
        for i in range(1, B):
            length = jnp.where(b == i, len_ref[i], length)
        score = lax.dot_general(kk, q[t], (((1,), (1,)), ((), ())), preferred_element_type=f32)
        cache = jnp.where(key_id < length, score[:keys] * scale, lowest)
        tree_seen = jnp.where(owner, reach[b], 0.0) > 0.5
        tree = jnp.where(tree_seen, score[keys:] * scale, lowest)
        top = jnp.maximum(
            jnp.max(cache, axis=0, keepdims=True), jnp.max(tree, axis=0, keepdims=True)
        )
        top = jnp.maximum(top, 0.1 * lowest)
        wc = jnp.exp2(cache - top)
        wt = jnp.exp2(tree - top)
        total = jnp.sum(wc, axis=0, keepdims=True) + jnp.sum(wt, axis=0, keepdims=True)
        w = jnp.concatenate([wc.astype(bf16), wt.astype(bf16)], axis=0)
        out = lax.dot_general(vv, w, (((0,), (0,)), ((), ())), preferred_element_type=f32)
        ml = jnp.concatenate(
            [jnp.broadcast_to(top, (4, R)), jnp.broadcast_to(total, (4, R))], axis=0
        )
        return out.astype(bf16), ml

    def remote(src, dst, ss, rs, dev):
        return pltpu.make_async_remote_copy(
            src_ref=src, dst_ref=dst, send_sem=ss, recv_sem=rs, device_id=dev, device_id_type=MESH
        )

    pl.semaphore_wait(barrier, S - 1 + H - 1)

    def send_chunk(i, carry):
        t = seq_peer(i)
        out, ml = chunk(t)
        o_send[t] = out
        ml_send[t] = ml
        remote(o_send.at[t], o_recv.at[s], o_ss.at[t], o_rs.at[s], (t, h)).start()
        remote(ml_send.at[t], ml_recv.at[s], ml_ss.at[t], ml_rs.at[s], (t, h)).start()
        return carry

    lax.fori_loop(1, S, send_chunk, 0)
    out, ml = chunk(s)
    o_recv[s] = out
    ml_recv[s] = ml

    for i in range(1, S):
        t = seq_peer(i)
        remote(o_send.at[t], o_recv.at[t], o_ss.at[t], o_rs.at[t], (t, h)).wait_recv()
        remote(ml_send.at[t], ml_recv.at[t], ml_ss.at[t], ml_rs.at[t], (t, h)).wait_recv()

    top = ml_recv[0, 0:1]
    for i in range(1, S):
        top = jnp.maximum(top, ml_recv[i, 0:1])
    total = jnp.zeros((1, R), f32)
    whole = jnp.zeros((HD, R), f32)
    for i in range(S):
        w = jnp.exp2(ml_recv[i, 0:1] - top)
        total += ml_recv[i, 4:5] * w
        whole += o_recv[i].astype(f32) * w
    att = jnp.transpose(whole / total).astype(bf16).reshape(heads_chunk, N, HD)

    def att_place(t):
        h0 = lax.rem(t, group) * heads_chunk
        return x_att.at[pl.ds(h0, heads_chunk), pl.ds(pl.multiple_of(t // group * N, N), N), :]

    a_send[...] = att
    x_att[
        pl.ds(lax.rem(s, group) * heads_chunk, heads_chunk),
        pl.ds(pl.multiple_of(s // group * N, N), N),
        :,
    ] = att
    a_sends = []
    for c, _, onward in att_plan:
        si = at_offset(c)[0]
        if c:
            remote(att_place(si), att_place(si), a_ss.at[0], a_rs.at[si], (s, h)).wait_recv()
        for n in onward:
            src = att_place(si) if c else a_send
            to = at_offset([n])[0]
            copy = remote(src, att_place(si), a_ss.at[len(a_sends)], a_rs.at[si], (to, h))
            copy.start()
            a_sends.append(copy)
    loads[5].wait()
    loads[6].wait()

    lhs = jnp.concatenate([x_att[i] for i in range(x_att.shape[0])], axis=1)
    proj = jnp.dot(lhs, ow[...], preferred_element_type=f32)
    for j in range(H):
        p_send[j] = proj[j * HR : (j + 1) * HR].astype(bf16)
    for i in range(1, H):
        t = head_peer(i)
        remote(p_send.at[t], p_recv.at[h], p_ss.at[t], p_rs.at[h], (s, t)).start()
    my_rows = pl.ds(pl.multiple_of(h * HR, HR), HR)
    stream = res[my_rows, :].astype(f32) + p_send[h].astype(f32)
    for i in range(1, H):
        t = head_peer(i)
        remote(p_send.at[t], p_recv.at[t], p_ss.at[t], p_rs.at[t], (s, t)).wait_recv()
        stream += p_recv[t].astype(f32)
    g[s, my_rows, :] = (stream * gain_ref[...].astype(f32)[None, :]).astype(bf16)

    def block(si, hi):
        return g.at[si, pl.ds(pl.multiple_of(hi * HR, HR), HR), :]

    sends = []

    def pass_on(si, hi, dev):
        c = remote(block(si, hi), block(si, hi), g_ss.at[len(sends)], g_rs.at[si * H + hi], dev)
        c.start()
        sends.append(c)

    def arrive(si, hi):
        remote(block(si, hi), block(si, hi), g_ss.at[0], g_rs.at[si * H + hi], (s, h)).wait_recv()

    def event(c, onward):
        si, hi = at_offset(c)
        if c:
            arrive(si, hi)
        for n in onward:
            pass_on(si, hi, at_offset([n]))

    tiles = max(1, VL // 512)
    width = VL // tiles

    def product(n):
        vw_copy(n).wait()
        left = g[order[n]]

        def tile(c, carry):
            cols = pl.ds(pl.multiple_of(c * width, width), width)
            part = jnp.dot(left, vw[slab(order[n]), cols], preferred_element_type=f32)
            acc[:, cols] = part if n == 0 else acc[:, cols] + part
            return carry

        lax.fori_loop(0, tiles, tile, 0)

    event(*row_plan[0][::2])

    eye = lax.broadcasted_iota(jnp.int32, (rows, rows), 0) == lax.broadcasted_iota(
        jnp.int32, (rows, rows), 1
    )

    def to_row(col):
        return jnp.sum(jnp.where(eye, col, 0.0), axis=0, keepdims=True)

    def to_col(row):
        return jnp.sum(jnp.where(eye, row, 0.0), axis=1, keepdims=True)

    squares = jnp.sum(stream * stream, axis=1, keepdims=True)
    mine = lax.broadcasted_iota(jnp.int32, (HR, rows), 0) + h * HR == lax.broadcasted_iota(
        jnp.int32, (HR, rows), 1
    )
    square_row = jnp.sum(jnp.where(mine, squares, 0.0), axis=0, keepdims=True)
    ss_send[...] = jnp.broadcast_to(square_row, (8, rows))
    for i in range(1, S):
        t = seq_peer(i)
        remote(ss_send, ss_r1.at[s], s1_ss.at[t], s1_rs.at[s], (t, h)).start()
    ss_r1[s] = ss_send[...]

    def squares_on():
        for i in range(1, S):
            t = seq_peer(i)
            remote(ss_send, ss_r1.at[t], s1_ss.at[t], s1_rs.at[t], (t, h)).wait_recv()
        part = ss_r1[0]
        for i in range(1, S):
            part = part + ss_r1[i]
        ss_mid[...] = part
        ss_r2[h] = part
        for i in range(1, H):
            t = head_peer(i)
            remote(ss_mid, ss_r2.at[h], s2_ss.at[t], s2_rs.at[h], (s, t)).start()

    place = {c: n for n, (c, _, _) in enumerate(row_plan)}
    ready = [max(place[c | o] for o in xc) for c in slabs]
    done = 0
    for n in range(1, S * H):
        event(*row_plan[n][::2])
        if n == S * H // 4:
            squares_on()
        while done < S and ready[done] + 2 <= n:
            product(done)
            done += 1
    for n in range(done, S):
        product(n)

    for i in range(1, H):
        t = head_peer(i)
        remote(ss_mid, ss_r2.at[t], s2_ss.at[t], s2_rs.at[t], (s, t)).wait_recv()
    square_sum = ss_r2[0, 0:1]
    for i in range(1, H):
        square_sum = square_sum + ss_r2[i, 0:1]
    inverse = to_col(lax.rsqrt(square_sum / D + epsilon))
    logits = acc[...] * inverse
    acc[...] = logits
    local_top = jnp.max(logits, axis=1, keepdims=True)
    local_sum = jnp.sum(jnp.exp(logits - local_top), axis=1, keepdims=True)
    ids = lax.broadcasted_iota(jnp.int32, (rows, VL), 1) + (s * H + h) * VL
    drafts = jnp.concatenate([draft_ref[b : b + 1, :] for b in range(B)], axis=1)
    wanted = to_col(drafts.astype(f32)).astype(jnp.int32)
    picked = jnp.sum(jnp.where(ids == wanted, logits, 0.0), axis=1, keepdims=True)
    stat = [to_row(local_top), to_row(local_sum), to_row(picked)]

    def pack(stat):
        return jnp.concatenate(stat + [jnp.zeros((5, rows), f32)], axis=0)

    def merge(ref, count):
        top = ref[0, 0:1]
        for i in range(1, count):
            top = jnp.maximum(top, ref[i, 0:1])
        total = jnp.zeros((1, rows), f32)
        got = jnp.zeros((1, rows), f32)
        for i in range(count):
            total += ref[i, 1:2] * jnp.exp(ref[i, 0:1] - top)
            got += ref[i, 2:3]
        return [top, total, got]

    st_send[...] = pack(stat)
    for i in range(1, S):
        t = seq_peer(i)
        remote(st_send, st_r1.at[s], t1_ss.at[t], t1_rs.at[s], (t, h)).start()
    st_r1[s] = pack(stat)
    for b in range(B):
        for i in range(path_ref.shape[1]):
            path_out[b, i : i + 1, :] = acc[pl.ds(path_ref[b, i] + b * N, 1), :]
    for i in range(1, S):
        t = seq_peer(i)
        remote(st_send, st_r1.at[t], t1_ss.at[t], t1_rs.at[t], (t, h)).wait_recv()
    both = pack(merge(st_r1, S))
    st_mid[...] = both
    st_r2[h] = both
    for i in range(1, H):
        t = head_peer(i)
        remote(st_mid, st_r2.at[h], t2_ss.at[t], t2_rs.at[h], (s, t)).start()
    for i in range(1, H):
        t = head_peer(i)
        remote(st_mid, st_r2.at[t], t2_ss.at[t], t2_rs.at[t], (s, t)).wait_recv()
    top, total, got = merge(st_r2, H)
    logp = got - (top + jnp.log(total))
    for b in range(B):
        logp_out[b : b + 1, :] = logp[:, b * N : (b + 1) * N]

    for i in range(1, S):
        t = seq_peer(i)
        remote(o_send.at[t], o_recv.at[s], o_ss.at[t], o_rs.at[s], (t, h)).wait_send()
        remote(ml_send.at[t], ml_recv.at[s], ml_ss.at[t], ml_rs.at[s], (t, h)).wait_send()
        remote(ss_send, ss_r1.at[s], s1_ss.at[t], s1_rs.at[s], (t, h)).wait_send()
        remote(st_send, st_r1.at[s], t1_ss.at[t], t1_rs.at[s], (t, h)).wait_send()
    for i in range(1, H):
        t = head_peer(i)
        remote(p_send.at[t], p_recv.at[h], p_ss.at[t], p_rs.at[h], (s, t)).wait_send()
        remote(ss_mid, ss_r2.at[h], s2_ss.at[t], s2_rs.at[h], (s, t)).wait_send()
        remote(st_mid, st_r2.at[h], t2_ss.at[t], t2_rs.at[h], (s, t)).wait_send()
    for c in a_sends + sends:
        c.wait_send()


def on_device(
    S,
    H,
    queries,
    cache_keys,
    cache_values,
    new_keys,
    new_values,
    parents,
    path,
    lengths,
    draft_tokens,
    residual,
    out_weight,
    norm_gain,
    vocab_weight,
):
    B, heads, N, HD = queries.shape
    KV, keys = cache_keys.shape[1], cache_keys.shape[2]
    BK = B * KV
    R = B * heads * N // S
    rows = B * N
    DL = out_weight.shape[1]
    D, VL = vocab_weight.shape
    K = out_weight.shape[0]
    HR = rows // H
    passes = S * H - 1
    vmem = pl.BlockSpec(memory_space=pltpu.VMEM)
    smem = pl.BlockSpec(memory_space=pltpu.SMEM)
    hbm = pl.BlockSpec(memory_space=pl.ANY)
    dma = pltpu.SemaphoreType.DMA
    path_logits, logp = pl.pallas_call(
        functools.partial(kernel, S, H, B, N, D),
        out_shape=(
            jax.ShapeDtypeStruct((B, path.shape[1], VL), f32),
            jax.ShapeDtypeStruct((B, N), f32),
        ),
        in_specs=[smem, smem, vmem, vmem, vmem] + [hbm] * 8,
        out_specs=(vmem, vmem),
        scratch_shapes=[
            pltpu.VMEM((S, R, HD), bf16),
            pltpu.VMEM((BK, keys + N, HD), bf16),
            pltpu.VMEM((BK, keys + N, HD), bf16),
            pltpu.VMEM((rows, DL), bf16),
            pltpu.VMEM((K, DL), bf16),
            pltpu.VMEM((D, VL), bf16),
            pltpu.VMEM((B, N, R), f32),
            pltpu.VMEM((S, HD, R), bf16),
            pltpu.VMEM((S, 8, R), f32),
            pltpu.VMEM((S, HD, R), bf16),
            pltpu.VMEM((S, 8, R), f32),
            pltpu.VMEM((R // N, N, HD), bf16),
            pltpu.VMEM((heads, rows, HD), bf16),
            pltpu.VMEM((H, HR, DL), bf16),
            pltpu.VMEM((H, HR, DL), bf16),
            pltpu.VMEM((S, rows, DL), bf16),
            pltpu.VMEM((rows, VL), f32),
            pltpu.VMEM((8, rows), f32),
            pltpu.VMEM((S, 8, rows), f32),
            pltpu.VMEM((8, rows), f32),
            pltpu.VMEM((H, 8, rows), f32),
            pltpu.VMEM((8, rows), f32),
            pltpu.VMEM((S, 8, rows), f32),
            pltpu.VMEM((8, rows), f32),
            pltpu.VMEM((H, 8, rows), f32),
            dma((7,)),
            dma((S,)),
            dma((S,)), dma((S,)), dma((S,)), dma((S,)), dma((S,)), dma((S,)),
            dma((H,)), dma((H,)),
            dma((passes,)), dma((S * H,)),
            dma((S,)), dma((S,)), dma((H,)), dma((H,)),
            dma((S,)), dma((S,)), dma((H,)), dma((H,)),
        ],
        compiler_params=pltpu.CompilerParams(
            collective_id=0, has_side_effects=True, vmem_limit_bytes=62 * 1024 * 1024
        ),
        name="verify",
    )(
        lengths,
        path,
        parents,
        draft_tokens,
        norm_gain,
        queries.reshape(S, R, HD),
        cache_keys.reshape(BK, keys, HD),
        cache_values.reshape(BK, keys, HD),
        new_keys.reshape(BK, N, HD),
        new_values.reshape(BK, N, HD),
        residual.reshape(rows, DL),
        out_weight,
        vocab_weight,
    )
    return path_logits, logp


def solution(mesh):
    placed = (
        P(None, "head", None, None),
        P(None, "head", "seq", None),
        P(None, "head", "seq", None),
        P(None, "head", None, None),
        P(None, "head", None, None),
        P(),
        P(),
        P(),
        P(),
        P(None, None, "seq"),
        P("head", "seq"),
        P("seq"),
        P(None, ("seq", "head")),
    )
    return jax.shard_map(
        functools.partial(on_device, mesh.shape["seq"], mesh.shape["head"]),
        mesh=mesh,
        in_specs=placed,
        out_specs=(P(None, None, ("seq", "head")), P()),
        check_vma=False,
    )
```
